32 devices in a mesh: groups: 2 (over x), ctx: 16 (over z, y, core).
Axes of the slice: x: 2, y: 2, z: 4, core: 2. Of those that a mesh axis runs over, the one named last changes fastest.
Arguments:
- context_keys: bfloat16 [4096, 2048], P(('groups', 'ctx')), parts along dimension 0, may hold values from -6 to 6
- context_values: bfloat16 [4096, 2048], P(('groups', 'ctx')), parts along dimension 0, may hold values from -6 to 6
- context_queries: bfloat16 [4096, 2048], P(('groups', 'ctx')), parts along dimension 0, may hold values from -6 to 6
- token_rates: float32 [8, 4096], P(None, ('groups', 'ctx')), parts along dimension 1, may hold values from 0.05 to 1
- w_gate: bfloat16 [8, 256, 256], replicated, may hold values from -0.375 to 0.375
- w_up: bfloat16 [8, 256, 256], replicated, may hold values from -0.375 to 0.375
- w_down: bfloat16 [8, 256, 256], replicated, may hold values from -0.375 to 0.375
- question_rows: bfloat16 [8192, 2048], P(('groups', 'ctx')), parts along dimension 0, may hold values from -6 to 6
- question_count: int32 [32], P(('groups', 'ctx')), parts along dimension 0, may hold values from 1 to 256, 1024 in all
Outputs:
- context_out: bfloat16 [4096, 2048], P(('groups', 'ctx')), parts along dimension 0
- answers: bfloat16 [8192, 2048], P(('groups', 'ctx')), parts along dimension 0
The draws below stay inside these ranges and needn't reach their ends.
There are 2 independent parts, one for each index of `groups`. The reference program is written for one: setup_inputs(seed, part) draws one part's arguments, and reference() takes and returns one part's arrays. A program takes and returns all parts, laid end to end along the dimension named above; an argument that names none is the same for every part. Nothing has to cross between parts.
Inputs may be any that keep to these rules, and one draw needn't show every extreme that they name: `question_count`: live rows are the first of each device's 256 slots. The counts of one user (the devices along ctx) add up to exactly 1024, and some device of each user has exactly 256.
All inputs are finite; a program needn't handle non-finite values.
Results may differ from the reference program's by a relative error of at most 0.018.
Values may be sent and summed in bfloat16 or wider, within the bound.
A program may use at most 128 MiB of HBM per device.

```python
import math
import jax
import jax.numpy as jnp
import numpy as np
from jax import lax

HEADS = 8
D_HEAD = 256
NS_STEPS = 3
Q_CAP = 256
Q_MEAN = 64
WIDTH = 2048
TOKENS = 2048
Q_ROWS = 4096
N_CTX = 16


def block_scale(own_key, dims, shards, least, high):
    loudness = 1.0
    for position, blocks in shards:
        draws = jax.random.uniform(jax.random.fold_in(jax.random.fold_in(own_key, 6), position), (blocks,), jnp.float32, least / len(shards), high / len(shards))
        loudness = loudness * jnp.repeat(jnp.exp(draws), dims[position] // blocks).reshape((-1,) + (1,) * (len(dims) - 1 - position))
    return loudness


def profile(amount, total, limit, skew):
    weights = [(1 << 20) // math.isqrt(rank ** skew) + 1 for rank in range(2, amount + 1)]
    rest, given = total - limit - (amount - 1), [1] * (amount - 1)
    while rest > 0:
        candidates = [i for i in range(amount - 1) if given[i] < limit]
        pool, left = sum([weights[i] for i in candidates]), rest
        for i in candidates:
            extra = min(limit - given[i], max(1, left * weights[i] // pool), rest)
            given[i] = given[i] + extra
            rest = rest - extra
    return np.array([limit] + given)


def ragged_sizes(stream_key, amount, total, reach, skew):
    if amount == 2:
        one = jax.random.randint(stream_key, (), max(1, total - reach), min(reach, total - 1) + 1)
        return jnp.stack([one, total - one])
    sizes = jnp.asarray(profile(amount, total, reach, skew), jnp.int32)
    pairs = (amount - 1) // 2
    donor, receiver = sizes[1:1 + 2 * pairs:2], sizes[2:2 + 2 * pairs:2]
    margin = jnp.minimum(donor - 1, reach - receiver)
    shifted = jax.random.randint(jax.random.fold_in(stream_key, 1), (pairs,), 0, 1 << 20) % (margin + 1)
    sizes = sizes.at[1:1 + 2 * pairs:2].set(donor - shifted).at[2:2 + 2 * pairs:2].set(receiver + shifted)
    return sizes[jax.random.permutation(jax.random.fold_in(stream_key, 2), amount)]


def gaussian(key, extent, spread, bound, split=(), held_as=jnp.bfloat16):
    drawn = spread * jax.random.normal(key, extent, jnp.float32)
    if split:
        drawn = drawn * block_scale(key, extent, split, -0.22, 0.18)
    return jnp.clip(drawn, -bound, bound).astype(held_as)


def setup_inputs(seed: int = 0, part: int = 0) -> dict:
    key_of = jax.random.split(jax.random.key(seed), 10)
    part_keys = jax.random.split(jax.random.fold_in(key_of[9], part), 10)
    context_keys = gaussian(part_keys[0], (TOKENS, WIDTH), 1.0, 6.0, ((0, 16),))
    context_values = gaussian(part_keys[1], (TOKENS, WIDTH), 1.0, 6.0, ((0, 16),))
    context_queries = gaussian(part_keys[2], (TOKENS, WIDTH), 1.0, 6.0, ((0, 16),))
    token_rates = jnp.clip(jnp.exp(math.log(1.0) - 2.9957323 * jax.random.uniform(part_keys[3], (HEADS, TOKENS), jnp.float32) ** block_scale(part_keys[3], (HEADS, TOKENS), ((1, 16),), -0.2, 0.2)), 0.05, 1.0)
    w_gate = gaussian(key_of[4], (HEADS, D_HEAD, D_HEAD), D_HEAD ** -0.5, 0.375)
    w_up = gaussian(key_of[5], (HEADS, D_HEAD, D_HEAD), D_HEAD ** -0.5, 0.375)
    w_down = gaussian(key_of[6], (HEADS, D_HEAD, D_HEAD), D_HEAD ** -0.5, 0.375)
    question_rows = gaussian(part_keys[7], (Q_ROWS, WIDTH), 1.0, 6.0, ((0, 16),))
    question_count = ragged_sizes(part_keys[8], N_CTX, Q_MEAN * N_CTX, Q_CAP, 2).astype(jnp.int32)
    return {"context_keys": context_keys, "context_values": context_values, "context_queries": context_queries, "token_rates": token_rates, "w_gate": w_gate, "w_up": w_up, "w_down": w_down, "question_rows": question_rows, "question_count": question_count}


quintic_first = 3.4445
quintic_second = -4.775
quintic_third = 2.0315

def apply_memory(in_rows, w_gate, w_up, w_down):
    head_size = w_gate.shape[1]
    pieces = []
    for head_index in range(w_gate.shape[0]):
        key_block = in_rows[:, head_index * head_size:(head_index + 1) * head_size]
        pre_gate = jnp.dot(key_block, w_gate[head_index], preferred_element_type=jnp.float32)
        pre_up = jnp.dot(key_block, w_up[head_index], preferred_element_type=jnp.float32)
        hidden = (jax.nn.silu(pre_gate) * pre_up).astype(jnp.bfloat16)
        pieces.append(jnp.dot(hidden, w_down[head_index], preferred_element_type=jnp.float32).astype(jnp.bfloat16))
    return jnp.concatenate(pieces, axis=1)

def memory_directions(context_keys, context_values, token_rates, w_gate, w_up, w_down):
    head_size = w_gate.shape[1]
    gate_list = []
    up_list = []
    down_list = []
    for head_index in range(w_gate.shape[0]):
        key_block = context_keys[:, head_index * head_size:(head_index + 1) * head_size]
        value_block = context_values[:, head_index * head_size:(head_index + 1) * head_size]
        pre_gate = jnp.dot(key_block, w_gate[head_index], preferred_element_type=jnp.float32)
        pre_up = jnp.dot(key_block, w_up[head_index], preferred_element_type=jnp.float32)
        sigmoid_gate = jax.nn.sigmoid(pre_gate)
        activated = pre_gate * sigmoid_gate
        hidden = (activated * pre_up).astype(jnp.bfloat16)
        weighted = (token_rates[head_index][:, None] * value_block.astype(jnp.float32)).astype(jnp.bfloat16)
        back_hidden = jnp.dot(weighted, w_down[head_index].T, preferred_element_type=jnp.float32)
        back_gate = (back_hidden * pre_up * sigmoid_gate * (1.0 + pre_gate * (1.0 - sigmoid_gate))).astype(jnp.bfloat16)
        back_up = (back_hidden * activated).astype(jnp.bfloat16)
        gate_list.append(jnp.dot(key_block.T, back_gate, preferred_element_type=jnp.float32))
        up_list.append(jnp.dot(key_block.T, back_up, preferred_element_type=jnp.float32))
        down_list.append(jnp.dot(hidden.T, weighted, preferred_element_type=jnp.float32))
    return jnp.stack([jnp.stack(gate_list), jnp.stack(up_list), jnp.stack(down_list)])

def reference(context_keys, context_values, context_queries, token_rates, w_gate, w_up, w_down, question_rows, question_count):
    context_out = apply_memory(context_queries, w_gate, w_up, w_down)
    direction = memory_directions(context_keys, context_values, token_rates, w_gate, w_up, w_down)
    stacked = direction.reshape(3 * HEADS, D_HEAD, D_HEAD)
    norm_sizes = jnp.sqrt(lax.optimization_barrier(jnp.sum(stacked * stacked, axis=(1, 2), keepdims=True)))
    iterate = (stacked / (norm_sizes + 1e-06)).astype(jnp.bfloat16)
    for sweep_index in range(NS_STEPS):
        wide = iterate.astype(jnp.float32)
        gram_matrix = jnp.einsum('mij,mkj->mik', wide, wide).astype(jnp.bfloat16)
        gram_wide = gram_matrix.astype(jnp.float32)
        gram_square = jnp.einsum('mij,mjk->mik', gram_wide, gram_wide)
        polynomial = (quintic_second * gram_wide + quintic_third * gram_square).astype(jnp.bfloat16)
        iterate = (quintic_first * wide + jnp.einsum('mij,mjk->mik', polynomial.astype(jnp.float32), wide)).astype(jnp.bfloat16)
    previous = jnp.stack([w_gate, w_up, w_down]).astype(jnp.float32)
    moved = previous + iterate.reshape(3, HEADS, D_HEAD, D_HEAD).astype(jnp.float32)
    col_norms = jnp.sqrt(lax.optimization_barrier(jnp.sum(previous * previous, axis=2, keepdims=True)))
    updated = (moved * col_norms / jnp.sqrt(lax.optimization_barrier(jnp.sum(moved * moved, axis=2, keepdims=True)) + 1e-06)).astype(jnp.bfloat16)
    outputs = apply_memory(question_rows, updated[0], updated[1], updated[2])
    positions = jnp.arange(Q_ROWS) % Q_CAP
    limits = jnp.repeat(question_count, Q_CAP)
    answers = jnp.where((positions < limits)[:, None], outputs, jnp.zeros_like(outputs))
    return (context_out, answers)
```

```python
import functools

import jax
import jax.numpy as jnp
from jax import lax
from jax.experimental import pallas as pl
from jax.experimental.pallas import tpu as pltpu
from jax.sharding import PartitionSpec as P

NS_STEPS = 3


quintic_first = 3.4445
quintic_second = -4.775
quintic_third = 2.0315


def fast_apply(in_rows, w_gate, w_up, w_down):
    head_count = w_gate.shape[0]
    head_size = w_gate.shape[1]
    row_split = in_rows.reshape(in_rows.shape[0], head_count, head_size)
    pre_gate = jnp.einsum("thd,hde->hte", row_split, w_gate, preferred_element_type=jnp.float32)
    pre_up = jnp.einsum("thd,hde->hte", row_split, w_up, preferred_element_type=jnp.float32)
    hidden = (jax.nn.silu(pre_gate) * pre_up).astype(jnp.bfloat16)
    outputs = jnp.einsum("hte,hef->thf", hidden, w_down, preferred_element_type=jnp.float32)
    return outputs.reshape(in_rows.shape[0], head_count * head_size).astype(jnp.bfloat16)


def directions(context_keys, context_values, token_rates, w_gate, w_up, w_down):
    tok_rows = context_keys.shape[0]
    head_count = w_gate.shape[0]
    head_size = w_gate.shape[1]
    key_split = context_keys.reshape(tok_rows, head_count, head_size)
    value_split = context_values.reshape(tok_rows, head_count, head_size)
    pre_gate = jnp.einsum("thd,hde->hte", key_split, w_gate, preferred_element_type=jnp.float32)
    pre_up = jnp.einsum("thd,hde->hte", key_split, w_up, preferred_element_type=jnp.float32)
    sigmoid_gate = jax.nn.sigmoid(pre_gate)
    activated = pre_gate * sigmoid_gate
    hidden = (activated * pre_up).astype(jnp.bfloat16)
    weighted = (token_rates.T[:, :, None] * value_split).astype(jnp.bfloat16)
    back_hidden = jnp.einsum("thf,hef->hte", weighted, w_down, preferred_element_type=jnp.float32)
    back_gate = (
        back_hidden * pre_up * sigmoid_gate * (1.0 + pre_gate * (1.0 - sigmoid_gate))
    ).astype(jnp.bfloat16)
    back_up = (back_hidden * activated).astype(jnp.bfloat16)
    step_gate = jnp.einsum("thd,hte->hde", key_split, back_gate, preferred_element_type=jnp.float32)
    step_up = jnp.einsum("thd,hte->hde", key_split, back_up, preferred_element_type=jnp.float32)
    step_down = jnp.einsum("hte,thf->hef", hidden, weighted, preferred_element_type=jnp.float32)
    return jnp.stack([step_gate, step_up, step_down])


def per_device(
    context_keys,
    context_values,
    context_queries,
    token_rates,
    w_gate,
    w_up,
    w_down,
    question_rows,
    question_count,
):
    head_count = w_gate.shape[0]
    head_size = w_gate.shape[1]
    matrix_count = 3 * head_count
    context_out = fast_apply(context_queries, w_gate, w_up, w_down)
    direction = directions(context_keys, context_values, token_rates, w_gate, w_up, w_down)
    flat_grads = direction.reshape(matrix_count, head_size * head_size)
    total = lax.psum(flat_grads, "ctx")
    norm_sizes = jnp.sqrt(jnp.sum(total * total, axis=1, keepdims=True))
    scaled = (total / (norm_sizes + 1e-06)).astype(jnp.bfloat16)
    iterate = scaled.reshape(matrix_count, head_size, head_size)
    for sweep_index in range(NS_STEPS):
        gram_matrix = jnp.einsum(
            "mij,mkj->mik", iterate, iterate, preferred_element_type=jnp.float32
        ).astype(jnp.bfloat16)
        gram_square = jnp.einsum(
            "mij,mjk->mik", gram_matrix, gram_matrix, preferred_element_type=jnp.float32
        )
        polynomial = (
            quintic_second * gram_matrix.astype(jnp.float32) + quintic_third * gram_square
        ).astype(jnp.bfloat16)
        product = jnp.einsum(
            "mij,mjk->mik", polynomial, iterate, preferred_element_type=jnp.float32
        )
        iterate = (quintic_first * iterate.astype(jnp.float32) + product).astype(jnp.bfloat16)
    previous = jnp.stack([w_gate, w_up, w_down]).astype(jnp.float32)
    moved = previous + iterate.reshape(3, head_count, head_size, head_size).astype(jnp.float32)
    col_norms = jnp.sqrt(jnp.sum(previous * previous, axis=2, keepdims=True))
    updated = (
        moved * col_norms / jnp.sqrt(jnp.sum(moved * moved, axis=2, keepdims=True) + 1e-06)
    ).astype(jnp.bfloat16)
    capacity = question_rows.shape[0]
    outputs = fast_apply(question_rows, updated[0], updated[1], updated[2])
    live_mask = jnp.arange(capacity, dtype=jnp.int32) < question_count[0]
    answers = jnp.where(live_mask[:, None], outputs, jnp.zeros_like(outputs))
    return (context_out, answers)


MESH = pl.DeviceIdType.MESH
ROWS = 2


def dot(a, b, contract=((1,), (0,))):
    return lax.dot_general(a, b, (contract, ((), ())), preferred_element_type=jnp.float32)


def read_memory(rows, gate, up, down):
    pre_gate = dot(rows, gate)
    pre_up = dot(rows, up)
    hidden = (pre_gate * jax.nn.sigmoid(pre_gate) * pre_up).astype(jnp.bfloat16)
    return dot(hidden, down).astype(jnp.bfloat16)


def memory_kernel(
    lines,
    keys_hbm, values_ref, queries_hbm, rates_ref, gate_hbm, up_hbm, down_hbm, questions_hbm,
    context_ref, answers_ref,
    key_in, weighted_in, weighted_out, queries, gate, up, down, questions, acc, other_acc, gathered,
    local_sem, key_send, key_recv, val_send, val_recv, acc_send, acc_recv,
    up_send, down_send, cross_send, pair_send, line_recv, pair_recv,
):
    heads, size, _ = gate.shape
    me = lax.axis_index("ctx")
    core, chip = me % ROWS, me // ROWS
    y, z = chip % ROWS, chip // ROWS
    half = ROWS * size * 3 // 4

    def device(a_chip, a_core):
        return {"ctx": a_chip * ROWS + a_core}

    def place(j):
        return (z // 2 + j // 2) % (lines // 2) * 2 + (z + j) % 2

    def columns(head):
        return pl.ds(pl.multiple_of(head * size, size), size)

    barrier = pltpu.get_barrier_semaphore()
    for j in range(lines):
        for dy in range(ROWS):
            if j or dy:
                peer = place(j) * ROWS + (y + dy) % ROWS
                pl.semaphore_signal(barrier, inc=1, device_id=device(peer, core), device_id_type=MESH)
    pl.semaphore_signal(barrier, inc=1, device_id=device(chip, 1 - core), device_id_type=MESH)

    loads = [
        pltpu.make_async_copy(src, dst, local_sem.at[i])
        for i, (src, dst) in enumerate([
            (gate_hbm, gate), (up_hbm, up), (down_hbm, down),
            (queries_hbm, queries), (questions_hbm, questions),
            (keys_hbm.at[:, columns(chip)], key_in.at[chip]),
        ])
    ]
    for load in loads:
        load.start()

    rates = rates_ref[...].T
    for head in range(heads):
        cols = slice(head * size, (head + 1) * size)
        weighted_out[head] = (
            rates[:, head:head + 1] * values_ref[:, cols].astype(jnp.float32)
        ).astype(jnp.bfloat16)
    own_weighted = pltpu.make_async_copy(weighted_out.at[chip], weighted_in.at[chip], local_sem.at[6])

    pl.semaphore_wait(barrier, lines * ROWS)
    own_weighted.start()

    def key_copy(to, slot):
        return pltpu.make_async_remote_copy(
            src_ref=keys_hbm.at[:, columns(to)], dst_ref=key_in.at[slot],
            send_sem=key_send.at[to], recv_sem=key_recv.at[slot],
            device_id=device(to, core), device_id_type=MESH)

    def val_copy(to, slot):
        return pltpu.make_async_remote_copy(
            src_ref=weighted_out.at[to], dst_ref=weighted_in.at[slot],
            send_sem=val_send.at[to], recv_sem=val_recv.at[slot],
            device_id=device(to, core), device_id_type=MESH)

    for j in reversed(range(lines)):
        for dy in range(ROWS):
            if j or dy:
                to = place(j) * ROWS + (y + dy) % ROWS
                key_copy(to, chip).start()
                val_copy(to, chip).start()

    for load in loads[:4]:
        load.wait()

    @pl.loop(0, heads)
    def _(head):
        context_ref[:, columns(head)] = read_memory(
            queries[:, columns(head)], gate[head], up[head], down[head])

    loads[5].wait()
    own_weighted.wait()
    acc[...] = jnp.zeros_like(acc)

    @pl.loop(0, lines)
    def _(j):
        line = place(j)
        for a_row in range(ROWS):
            source = line * ROWS + a_row

            @pl.when(source != chip)
            def _():
                key_copy(source, source).wait_recv()
                val_copy(source, source).wait_recv()

        pair = pl.ds(line * ROWS, ROWS)
        key = key_in[pair].reshape(-1, size)
        weighted = weighted_in[pair].reshape(-1, size)
        pre_gate = dot(key, gate[chip])
        pre_up = dot(key, up[chip])
        back_hidden = dot(weighted, down[chip], ((1,), (1,)))
        sigmoid = jax.nn.sigmoid(pre_gate)
        active = pre_gate * sigmoid
        hidden = (active * pre_up).astype(jnp.bfloat16)
        back_gate = (
            back_hidden * pre_up * sigmoid * (1.0 + pre_gate * (1.0 - sigmoid))
        ).astype(jnp.bfloat16)
        back_up = (back_hidden * active).astype(jnp.bfloat16)
        acc[0] += dot(key, back_gate, ((0,), (0,)))
        acc[1] += dot(key, back_up, ((0,), (0,)))
        acc[2] += dot(hidden, weighted, ((0,), (0,)))

    exchange = pltpu.make_async_remote_copy(
        src_ref=acc, dst_ref=other_acc, send_sem=acc_send, recv_sem=acc_recv,
        device_id=device(chip, 1 - core), device_id_type=MESH)
    exchange.start()
    exchange.wait()

    matrices = []
    for m in range(3):
        total = acc[m] + other_acc[m]
        norm = jnp.sqrt(jnp.sum(total * total, keepdims=True))
        matrices.append((total / (norm + 1e-06)).astype(jnp.bfloat16))
    for _ in range(NS_STEPS):
        grams = [dot(x, x, ((1,), (1,))).astype(jnp.bfloat16) for x in matrices]
        polys = [
            (quintic_second * g.astype(jnp.float32) + quintic_third * dot(g, g)).astype(jnp.bfloat16)
            for g in grams
        ]
        matrices = [
            (quintic_first * x.astype(jnp.float32) + dot(p, x)).astype(jnp.bfloat16)
            for p, x in zip(polys, matrices)
        ]
    for m, (initial, x) in enumerate(zip((gate, up, down), matrices)):
        previous = initial[chip].astype(jnp.float32)
        moved = previous + x.astype(jnp.float32)
        norms = jnp.sqrt(jnp.sum(previous * previous, axis=0, keepdims=True))
        gathered[chip, m * size:(m + 1) * size, :] = (
            moved * norms / jnp.sqrt(jnp.sum(moved * moved, axis=0, keepdims=True) + 1e-06)
        ).astype(jnp.bfloat16)

    def hop(origin, part, send, recv, to_chip, to_core):
        block = gathered.at[origin, pl.ds(pl.multiple_of(part * half, half), half)]
        return pltpu.make_async_remote_copy(
            src_ref=block, dst_ref=block, send_sem=send.at[origin], recv_sem=recv.at[origin],
            device_id=device(to_chip, to_core), device_id_type=MESH)

    def hop_up(origin):
        return hop(origin, core, up_send, line_recv, chip + ROWS, core)

    def hop_down(origin):
        return hop(origin, core, down_send, line_recv, chip - ROWS, core)

    def hop_cross(origin):
        return hop(origin, core, cross_send, line_recv, z * ROWS + 1 - y, core)

    def hop_pair(origin):
        return hop(origin, core, pair_send, pair_recv, chip, 1 - core)

    def from_pair(origin):
        return hop(origin, 1 - core, pair_send, pair_recv, chip, 1 - core)

    def answer(origin):
        answers_ref[:, columns(origin)] = read_memory(
            questions[:, columns(origin)],
            gathered[origin, 0:size, :],
            gathered[origin, size:2 * size, :],
            gathered[origin, 2 * size:3 * size, :])

    @pl.when(z + 1 < lines)
    def _():
        hop_up(chip).start()

    @pl.when(z > 0)
    def _():
        hop_down(chip).start()

    hop_cross(chip).start()
    loads[4].wait()
    answer(chip)

    @pl.loop(1, lines + 2)
    def _(k):
        @pl.when(z - k >= 0)
        def _():
            origin = chip - ROWS * k
            hop_cross(origin).wait_recv()

            @pl.when(z + 1 < lines)
            def _():
                hop_up(origin).start()

            hop_cross(origin).start()
            hop_pair(origin).start()

        @pl.when(z + k < lines)
        def _():
            origin = chip + ROWS * k
            hop_cross(origin).wait_recv()

            @pl.when(z > 0)
            def _():
                hop_down(origin).start()

            hop_cross(origin).start()
            hop_pair(origin).start()

        def crossed(line):
            origin = line * ROWS + 1 - y
            hop_cross(origin).wait_recv()
            hop_pair(origin).start()

        def finish(origin):
            from_pair(origin).wait_recv()
            answer(origin)

        near = k - 1
        last = k - 2
        pl.when(z - near >= 0)(lambda: crossed(z - near))
        pl.when((near > 0) & (z + near < lines))(lambda: crossed(z + near))
        pl.when((near > 0) & (z - near >= 0))(lambda: finish((z - near) * ROWS + y))
        pl.when((near > 0) & (z + near < lines))(lambda: finish((z + near) * ROWS + y))
        pl.when((last >= 0) & (z - last >= 0))(lambda: finish((z - last) * ROWS + 1 - y))
        pl.when((last > 0) & (z + last < lines))(lambda: finish((z + last) * ROWS + 1 - y))

    @pl.loop(0, lines)
    def _(line):
        mine = line * ROWS + y
        across = line * ROWS + 1 - y
        pl.when((line <= z) & (z + 1 < lines))(lambda: hop_up(mine).wait_send())
        pl.when((line >= z) & (z > 0))(lambda: hop_down(mine).wait_send())
        hop_cross(mine).wait_send()
        hop_pair(across).wait_send()
        key_copy(across, across).wait_send()
        val_copy(across, across).wait_send()

        @pl.when(line != z)
        def _():
            hop_pair(mine).wait_send()
            key_copy(mine, mine).wait_send()
            val_copy(mine, mine).wait_send()


def head_per_chip(
    lines,
    context_keys,
    context_values,
    context_queries,
    token_rates,
    w_gate,
    w_up,
    w_down,
    question_rows,
    question_count,
):
    heads, size, _ = w_gate.shape
    tokens, width = context_keys.shape
    capacity = question_rows.shape[0]
    vmem = pl.BlockSpec(memory_space=pltpu.VMEM)
    anywhere = pl.BlockSpec(memory_space=pl.ANY)
    sem = pltpu.SemaphoreType.DMA
    half_type = jnp.bfloat16
    context_out, outputs = pl.pallas_call(
        functools.partial(memory_kernel, lines),
        out_shape=(
            jax.ShapeDtypeStruct((tokens, width), half_type),
            jax.ShapeDtypeStruct((capacity, width), half_type),
        ),
        in_specs=[anywhere, vmem, anywhere, vmem, anywhere, anywhere, anywhere, anywhere],
        out_specs=(vmem, vmem),
        scratch_shapes=[
            pltpu.VMEM((heads, tokens, size), half_type),
            pltpu.VMEM((heads, tokens, size), half_type),
            pltpu.VMEM((heads, tokens, size), half_type),
            pltpu.VMEM((tokens, width), half_type),
            pltpu.VMEM((heads, size, size), half_type),
            pltpu.VMEM((heads, size, size), half_type),
            pltpu.VMEM((heads, size, size), half_type),
            pltpu.VMEM((capacity, width), half_type),
            pltpu.VMEM((3, size, size), jnp.float32),
            pltpu.VMEM((3, size, size), jnp.float32),
            pltpu.VMEM((heads, 3 * size, size), half_type),
            sem((7,)),
            sem((heads,)), sem((heads,)), sem((heads,)), sem((heads,)),
            sem, sem,
            sem((heads,)), sem((heads,)), sem((heads,)), sem((heads,)),
            sem((heads,)), sem((heads,)),
        ],
        compiler_params=pltpu.CompilerParams(
            collective_id=0, has_side_effects=True, vmem_limit_bytes=48 * 1024 * 1024
        ),
    )(context_keys, context_values, context_queries, token_rates, w_gate, w_up, w_down, question_rows)
    live_mask = jnp.arange(capacity, dtype=jnp.int32) < question_count[0]
    return context_out, jnp.where(live_mask[:, None], outputs, jnp.zeros_like(outputs))


def solution(mesh):
    members = mesh.shape["ctx"]
    lines = members // (ROWS * ROWS)

    def body(*arrays):
        heads = arrays[4].shape[0]
        if members == ROWS * heads and lines % 2 == 0:
            return head_per_chip(lines, *arrays)
        return per_device(*arrays)

    return jax.shard_map(
        body,
        mesh=mesh,
        in_specs=(
            P(("groups", "ctx"), None),
            P(("groups", "ctx"), None),
            P(("groups", "ctx"), None),
            P(None, ("groups", "ctx")),
            P(),
            P(),
            P(),
            P(("groups", "ctx"), None),
            P(("groups", "ctx")),
        ),
        out_specs=(P(("groups", "ctx"), None), P(("groups", "ctx"), None)),
        check_vma=False,
    )
```

```python
import functools

import jax
import jax.numpy as jnp
from jax import lax
from jax.experimental import pallas as pl
from jax.experimental.pallas import tpu as pltpu
from jax.sharding import PartitionSpec as P

NS_STEPS = 3


quintic_first = 3.4445
quintic_second = -4.775
quintic_third = 2.0315


def fast_apply(in_rows, w_gate, w_up, w_down):
    head_count = w_gate.shape[0]
    head_size = w_gate.shape[1]
    row_split = in_rows.reshape(in_rows.shape[0], head_count, head_size)
    pre_gate = jnp.einsum("thd,hde->hte", row_split, w_gate, preferred_element_type=jnp.float32)
    pre_up = jnp.einsum("thd,hde->hte", row_split, w_up, preferred_element_type=jnp.float32)
    hidden = (jax.nn.silu(pre_gate) * pre_up).astype(jnp.bfloat16)
    outputs = jnp.einsum("hte,hef->thf", hidden, w_down, preferred_element_type=jnp.float32)
    return outputs.reshape(in_rows.shape[0], head_count * head_size).astype(jnp.bfloat16)


def directions(context_keys, context_values, token_rates, w_gate, w_up, w_down):
    tok_rows = context_keys.shape[0]
    head_count = w_gate.shape[0]
    head_size = w_gate.shape[1]
    key_split = context_keys.reshape(tok_rows, head_count, head_size)
    value_split = context_values.reshape(tok_rows, head_count, head_size)
    pre_gate = jnp.einsum("thd,hde->hte", key_split, w_gate, preferred_element_type=jnp.float32)
    pre_up = jnp.einsum("thd,hde->hte", key_split, w_up, preferred_element_type=jnp.float32)
    sigmoid_gate = jax.nn.sigmoid(pre_gate)
    activated = pre_gate * sigmoid_gate
    hidden = (activated * pre_up).astype(jnp.bfloat16)
    weighted = (token_rates.T[:, :, None] * value_split).astype(jnp.bfloat16)
    back_hidden = jnp.einsum("thf,hef->hte", weighted, w_down, preferred_element_type=jnp.float32)
    back_gate = (
        back_hidden * pre_up * sigmoid_gate * (1.0 + pre_gate * (1.0 - sigmoid_gate))
    ).astype(jnp.bfloat16)
    back_up = (back_hidden * activated).astype(jnp.bfloat16)
    step_gate = jnp.einsum("thd,hte->hde", key_split, back_gate, preferred_element_type=jnp.float32)
    step_up = jnp.einsum("thd,hte->hde", key_split, back_up, preferred_element_type=jnp.float32)
    step_down = jnp.einsum("hte,thf->hef", hidden, weighted, preferred_element_type=jnp.float32)
    return jnp.stack([step_gate, step_up, step_down])


def per_device(
    context_keys,
    context_values,
    context_queries,
    token_rates,
    w_gate,
    w_up,
    w_down,
    question_rows,
    question_count,
):
    head_count = w_gate.shape[0]
    head_size = w_gate.shape[1]
    matrix_count = 3 * head_count
    context_out = fast_apply(context_queries, w_gate, w_up, w_down)
    direction = directions(context_keys, context_values, token_rates, w_gate, w_up, w_down)
    flat_grads = direction.reshape(matrix_count, head_size * head_size)
    total = lax.psum(flat_grads, "ctx")
    norm_sizes = jnp.sqrt(jnp.sum(total * total, axis=1, keepdims=True))
    scaled = (total / (norm_sizes + 1e-06)).astype(jnp.bfloat16)
    iterate = scaled.reshape(matrix_count, head_size, head_size)
    for sweep_index in range(NS_STEPS):
        gram_matrix = jnp.einsum(
            "mij,mkj->mik", iterate, iterate, preferred_element_type=jnp.float32
        ).astype(jnp.bfloat16)
        gram_square = jnp.einsum(
            "mij,mjk->mik", gram_matrix, gram_matrix, preferred_element_type=jnp.float32
        )
        polynomial = (
            quintic_second * gram_matrix.astype(jnp.float32) + quintic_third * gram_square
        ).astype(jnp.bfloat16)
        product = jnp.einsum(
            "mij,mjk->mik", polynomial, iterate, preferred_element_type=jnp.float32
        )
        iterate = (quintic_first * iterate.astype(jnp.float32) + product).astype(jnp.bfloat16)
    previous = jnp.stack([w_gate, w_up, w_down]).astype(jnp.float32)
    moved = previous + iterate.reshape(3, head_count, head_size, head_size).astype(jnp.float32)
    col_norms = jnp.sqrt(jnp.sum(previous * previous, axis=2, keepdims=True))
    updated = (
        moved * col_norms / jnp.sqrt(jnp.sum(moved * moved, axis=2, keepdims=True) + 1e-06)
    ).astype(jnp.bfloat16)
    capacity = question_rows.shape[0]
    outputs = fast_apply(question_rows, updated[0], updated[1], updated[2])
    live_mask = jnp.arange(capacity, dtype=jnp.int32) < question_count[0]
    answers = jnp.where(live_mask[:, None], outputs, jnp.zeros_like(outputs))
    return (context_out, answers)


MESH = pl.DeviceIdType.MESH
PIECES = 2
ROWS = 2


def dot(a, b, contract=((1,), (0,))):
    return lax.dot_general(a, b, (contract, ((), ())), preferred_element_type=jnp.float32)


def read_memory(rows, gate, up, down):
    pre_gate = dot(rows, gate)
    pre_up = dot(rows, up)
    hidden = (pre_gate * jax.nn.sigmoid(pre_gate) * pre_up).astype(jnp.bfloat16)
    return dot(hidden, down).astype(jnp.bfloat16)


def memory_kernel(
    lines,
    keys_hbm, values_hbm, queries_hbm, rates_hbm, gate_hbm, up_hbm, down_hbm, questions_hbm,
    context_ref, answers_ref,
    key_in, weighted_in, weighted_out, values, rates_in, queries, gate, up, down, questions, acc, other_acc, gathered,
    local_sem, key_send, key_recv, val_send, val_recv, acc_send, acc_recv,
    up_send, down_send, cross_send, pair_send, line_recv, pair_recv,
):
    heads, size, _ = gate.shape
    me = lax.axis_index("ctx")
    core, chip = me % ROWS, me // ROWS
    y, z = chip % ROWS, chip // ROWS
    half = 3 * size // ROWS
    piece = half // PIECES

    def device(a_chip, a_core):
        return {"ctx": a_chip * ROWS + a_core}

    def place(j):
        return (z // 2 + j // 2) % (lines // 2) * 2 + (z + j) % 2

    def columns(head):
        return pl.ds(pl.multiple_of(head * size, size), size)

    barrier = pltpu.get_barrier_semaphore()
    for j in range(lines):
        for dy in range(ROWS):
            if j or dy:
                peer = place(j) * ROWS + (y + dy) % ROWS
                pl.semaphore_signal(barrier, inc=1, device_id=device(peer, core), device_id_type=MESH)
    pl.semaphore_signal(barrier, inc=1, device_id=device(chip, 1 - core), device_id_type=MESH)

    loads = [
        pltpu.make_async_copy(src, dst, local_sem.at[i])
        for i, (src, dst) in enumerate([
            (rates_hbm, rates_in), (values_hbm, values),
            (keys_hbm.at[:, columns(chip)], key_in.at[chip]),
            (queries_hbm, queries), (gate_hbm, gate), (up_hbm, up), (down_hbm, down),
            (questions_hbm, questions),
        ])
    ]
    for load in loads:
        load.start()

    loads[0].wait()
    loads[1].wait()
    rates = rates_in[...].T
    for head in range(heads):
        cols = slice(head * size, (head + 1) * size)
        weighted_out[head] = (
            rates[:, head:head + 1] * values[:, cols].astype(jnp.float32)
        ).astype(jnp.bfloat16)
    own_weighted = pltpu.make_async_copy(weighted_out.at[chip], weighted_in.at[chip], local_sem.at[8])

    pl.semaphore_wait(barrier, lines * ROWS)
    own_weighted.start()

    def key_copy(to, slot):
        return pltpu.make_async_remote_copy(
            src_ref=keys_hbm.at[:, columns(to)], dst_ref=key_in.at[slot],
            send_sem=key_send.at[to], recv_sem=key_recv.at[slot],
            device_id=device(to, core), device_id_type=MESH)

    def val_copy(to, slot):
        return pltpu.make_async_remote_copy(
            src_ref=weighted_out.at[to], dst_ref=weighted_in.at[slot],
            send_sem=val_send.at[to], recv_sem=val_recv.at[slot],
            device_id=device(to, core), device_id_type=MESH)

    for j in reversed(range(lines)):
        for dy in range(ROWS):
            if j or dy:
                to = place(j) * ROWS + (y + dy) % ROWS
                key_copy(to, chip).start()
                val_copy(to, chip).start()

    for load in loads[2:7]:
        load.wait()

    @pl.loop(0, heads)
    def _(head):
        context_ref[:, columns(head)] = read_memory(
            queries[:, columns(head)], gate[head], up[head], down[head])

    own_weighted.wait()
    acc[...] = jnp.zeros_like(acc)

    @pl.loop(0, lines)
    def _(j):
        line = place(j)
        for a_row in range(ROWS):
            source = line * ROWS + a_row

            @pl.when(source != chip)
            def _():
                key_copy(source, source).wait_recv()
                val_copy(source, source).wait_recv()

        pair = pl.ds(line * ROWS, ROWS)
        key = key_in[pair].reshape(-1, size)
        weighted = weighted_in[pair].reshape(-1, size)
        pre_gate = dot(key, gate[chip])
        pre_up = dot(key, up[chip])
        back_hidden = dot(weighted, down[chip], ((1,), (1,)))
        sigmoid = jax.nn.sigmoid(pre_gate)
        active = pre_gate * sigmoid
        hidden = (active * pre_up).astype(jnp.bfloat16)
        back_gate = (
            back_hidden * pre_up * sigmoid * (1.0 + pre_gate * (1.0 - sigmoid))
        ).astype(jnp.bfloat16)
        back_up = (back_hidden * active).astype(jnp.bfloat16)
        acc[0] += dot(key, back_gate, ((0,), (0,)))
        acc[1] += dot(key, back_up, ((0,), (0,)))
        acc[2] += dot(hidden, weighted, ((0,), (0,)))

    exchange = pltpu.make_async_remote_copy(
        src_ref=acc, dst_ref=other_acc, send_sem=acc_send, recv_sem=acc_recv,
        device_id=device(chip, 1 - core), device_id_type=MESH)
    exchange.start()
    exchange.wait()

    matrices = []
    for m in range(3):
        total = acc[m] + other_acc[m]
        norm = jnp.sqrt(jnp.sum(total * total, keepdims=True))
        matrices.append((total / (norm + 1e-06)).astype(jnp.bfloat16))
    for _ in range(NS_STEPS):
        grams = [dot(x, x, ((1,), (1,))).astype(jnp.bfloat16) for x in matrices]
        polys = [
            (quintic_second * g.astype(jnp.float32) + quintic_third * dot(g, g)).astype(jnp.bfloat16)
            for g in grams
        ]
        matrices = [
            (quintic_first * x.astype(jnp.float32) + dot(p, x)).astype(jnp.bfloat16)
            for p, x in zip(polys, matrices)
        ]
    for m, (initial, x) in enumerate(zip((gate, up, down), matrices)):
        previous = initial[chip].astype(jnp.float32)
        moved = previous + x.astype(jnp.float32)
        norms = jnp.sqrt(jnp.sum(previous * previous, axis=0, keepdims=True))
        gathered[chip, m * size:(m + 1) * size, :] = (
            moved * norms / jnp.sqrt(jnp.sum(moved * moved, axis=0, keepdims=True) + 1e-06)
        ).astype(jnp.bfloat16)

    def hop(origin, p, part, send, recv, to_chip, to_core):
        rows = pl.ds(pl.multiple_of(part * half + p * piece, piece), piece)
        block = gathered.at[origin, rows]
        slot = origin * PIECES + p
        return pltpu.make_async_remote_copy(
            src_ref=block, dst_ref=block, send_sem=send.at[slot], recv_sem=recv.at[slot],
            device_id=device(to_chip, to_core), device_id_type=MESH)

    def hop_up(origin, p):
        return hop(origin, p, core, up_send, line_recv, chip + ROWS, core)

    def hop_down(origin, p):
        return hop(origin, p, core, down_send, line_recv, chip - ROWS, core)

    def hop_cross(origin, p):
        return hop(origin, p, core, cross_send, line_recv, z * ROWS + 1 - y, core)

    def hop_pair(origin, p):
        return hop(origin, p, core, pair_send, pair_recv, chip, 1 - core)

    def from_pair(origin, p):
        return hop(origin, p, 1 - core, pair_send, pair_recv, chip, 1 - core)

    def answer(origin):
        answers_ref[:, columns(origin)] = read_memory(
            questions[:, columns(origin)],
            gathered[origin, 0:size, :],
            gathered[origin, size:2 * size, :],
            gathered[origin, 2 * size:3 * size, :])

    def early(line):
        return (core == 0) & ((line == 0) | (line == lines - 1))

    def late(line):
        return jnp.logical_not(early(line))

    has_up, has_down = z + 1 < lines, z > 0

    def mine(line):
        return line * ROWS + y

    def across(line):
        return line * ROWS + 1 - y

    for p in range(PIECES):
        hop_cross(chip, p).start()
        pl.when(has_up)(lambda: hop_up(chip, p).start())
        pl.when(has_down)(lambda: hop_down(chip, p).start())

    @pl.when(early(z))
    def _():
        for p in range(PIECES):
            hop_cross(across(z), p).wait_recv()
            pl.when(has_up)(lambda: hop_up(across(z), p).start())
            pl.when(has_down)(lambda: hop_down(across(z), p).start())
            hop_pair(across(z), p).start()

    loads[7].wait()
    answer(chip)

    def along(line, has_next, next_hop):
        for p in range(PIECES):
            origin = mine(line)
            hop_cross(origin, p).wait_recv()
            pl.when(has_next)(lambda: next_hop(origin, p).start())
            pl.when(late(line))(lambda: hop_cross(origin, p).start())
            hop_pair(origin, p).start()

        @pl.when(early(line))
        def _():
            for p in range(PIECES):
                hop_cross(across(line), p).wait_recv()
                pl.when(has_next)(lambda: next_hop(across(line), p).start())
                hop_pair(across(line), p).start()

    def crossed(line):
        @pl.when(late(line))
        def _():
            for p in range(PIECES):
                hop_cross(across(line), p).wait_recv()
                hop_pair(across(line), p).start()

    def finish(origin):
        for p in range(PIECES):
            from_pair(origin, p).wait_recv()
        answer(origin)

    @pl.loop(1, lines + 2)
    def _(k):
        pl.when(z - k >= 0)(lambda: along(z - k, has_up, hop_up))
        pl.when(z + k < lines)(lambda: along(z + k, has_down, hop_down))
        near = k - 1
        last = k - 2
        pl.when(z - near >= 0)(lambda: crossed(z - near))
        pl.when((near > 0) & (z + near < lines))(lambda: crossed(z + near))
        pl.when((near > 0) & (z - near >= 0))(lambda: finish(mine(z - near)))
        pl.when((near > 0) & (z + near < lines))(lambda: finish(mine(z + near)))
        pl.when((last >= 0) & (z - last >= 0))(lambda: finish(across(z - last)))
        pl.when((last > 0) & (z + last < lines))(lambda: finish(across(z + last)))

    @pl.loop(0, lines)
    def _(line):
        goes_up = (line <= z) & has_up
        goes_down = (line >= z) & has_down
        key_copy(across(line), across(line)).wait_send()
        val_copy(across(line), across(line)).wait_send()

        @pl.when(line != z)
        def _():
            key_copy(mine(line), mine(line)).wait_send()
            val_copy(mine(line), mine(line)).wait_send()

        for p in range(PIECES):
            pl.when(goes_up & early(line))(lambda: hop_up(across(line), p).wait_send())
            pl.when(goes_down & early(line))(lambda: hop_down(across(line), p).wait_send())
            pl.when(goes_up)(lambda: hop_up(mine(line), p).wait_send())
            pl.when(goes_down)(lambda: hop_down(mine(line), p).wait_send())
            pl.when(late(line) | (line == z))(lambda: hop_cross(mine(line), p).wait_send())
            hop_pair(across(line), p).wait_send()
            pl.when(line != z)(lambda: hop_pair(mine(line), p).wait_send())


def head_per_chip(
    lines,
    context_keys,
    context_values,
    context_queries,
    token_rates,
    w_gate,
    w_up,
    w_down,
    question_rows,
    question_count,
):
    heads, size, _ = w_gate.shape
    tokens, width = context_keys.shape
    capacity = question_rows.shape[0]
    vmem = pl.BlockSpec(memory_space=pltpu.VMEM)
    sem = pltpu.SemaphoreType.DMA
    half_type = jnp.bfloat16
    context_out, outputs = pl.pallas_call(
        functools.partial(memory_kernel, lines),
        out_shape=(
            jax.ShapeDtypeStruct((tokens, width), half_type),
            jax.ShapeDtypeStruct((capacity, width), half_type),
        ),
        in_specs=[pl.BlockSpec(memory_space=pltpu.HBM)] * 8,
        out_specs=(vmem, vmem),
        scratch_shapes=[
            pltpu.VMEM((heads, tokens, size), half_type),
            pltpu.VMEM((heads, tokens, size), half_type),
            pltpu.VMEM((heads, tokens, size), half_type),
            pltpu.VMEM((tokens, width), half_type),
            pltpu.VMEM((heads, tokens), jnp.float32),
            pltpu.VMEM((tokens, width), half_type),
            pltpu.VMEM((heads, size, size), half_type),
            pltpu.VMEM((heads, size, size), half_type),
            pltpu.VMEM((heads, size, size), half_type),
            pltpu.VMEM((capacity, width), half_type),
            pltpu.VMEM((3, size, size), jnp.float32),
            pltpu.VMEM((3, size, size), jnp.float32),
            pltpu.VMEM((heads, 3 * size, size), half_type),
            sem((9,)),
            sem((heads,)), sem((heads,)), sem((heads,)), sem((heads,)),
            sem, sem,
            *[sem((heads * PIECES,))] * 6,
        ],
        compiler_params=pltpu.CompilerParams(
            collective_id=0, has_side_effects=True, vmem_limit_bytes=48 * 1024 * 1024
        ),
    )(*(
        pltpu.with_memory_space_constraint(array, pltpu.HBM)
        for array in (
            context_keys, context_values, context_queries, token_rates,
            w_gate, w_up, w_down, question_rows,
        )
    ))
    live_mask = jnp.arange(capacity, dtype=jnp.int32) < question_count[0]
    return context_out, jnp.where(live_mask[:, None], outputs, jnp.zeros_like(outputs))


def solution(mesh):
    members = mesh.shape["ctx"]
    lines = members // (ROWS * ROWS)

    def body(*arrays):
        heads = arrays[4].shape[0]
        if members == ROWS * heads and lines % 2 == 0:
            return head_per_chip(lines, *arrays)
        return per_device(*arrays)

    return jax.shard_map(
        body,
        mesh=mesh,
        in_specs=(
            P(("groups", "ctx"), None),
            P(("groups", "ctx"), None),
            P(("groups", "ctx"), None),
            P(None, ("groups", "ctx")),
            P(),
            P(),
            P(),
            P(("groups", "ctx"), None),
            P(("groups", "ctx")),
        ),
        out_specs=(P(("groups", "ctx"), None), P(("groups", "ctx"), None)),
        check_vma=False,
    )
```

```python
import functools

import jax
import jax.numpy as jnp
from jax import lax
from jax.experimental import pallas as pl
from jax.experimental.pallas import tpu as pltpu
from jax.sharding import PartitionSpec as P

NS_STEPS = 3


quintic_first = 3.4445
quintic_second = -4.775
quintic_third = 2.0315


def fast_apply(in_rows, w_gate, w_up, w_down):
    head_count = w_gate.shape[0]
    head_size = w_gate.shape[1]
    row_split = in_rows.reshape(in_rows.shape[0], head_count, head_size)
    pre_gate = jnp.einsum("thd,hde->hte", row_split, w_gate, preferred_element_type=jnp.float32)
    pre_up = jnp.einsum("thd,hde->hte", row_split, w_up, preferred_element_type=jnp.float32)
    hidden = (jax.nn.silu(pre_gate) * pre_up).astype(jnp.bfloat16)
    outputs = jnp.einsum("hte,hef->thf", hidden, w_down, preferred_element_type=jnp.float32)
    return outputs.reshape(in_rows.shape[0], head_count * head_size).astype(jnp.bfloat16)


def directions(context_keys, context_values, token_rates, w_gate, w_up, w_down):
    tok_rows = context_keys.shape[0]
    head_count = w_gate.shape[0]
    head_size = w_gate.shape[1]
    key_split = context_keys.reshape(tok_rows, head_count, head_size)
    value_split = context_values.reshape(tok_rows, head_count, head_size)
    pre_gate = jnp.einsum("thd,hde->hte", key_split, w_gate, preferred_element_type=jnp.float32)
    pre_up = jnp.einsum("thd,hde->hte", key_split, w_up, preferred_element_type=jnp.float32)
    sigmoid_gate = jax.nn.sigmoid(pre_gate)
    activated = pre_gate * sigmoid_gate
    hidden = (activated * pre_up).astype(jnp.bfloat16)
    weighted = (token_rates.T[:, :, None] * value_split).astype(jnp.bfloat16)
    back_hidden = jnp.einsum("thf,hef->hte", weighted, w_down, preferred_element_type=jnp.float32)
    back_gate = (
        back_hidden * pre_up * sigmoid_gate * (1.0 + pre_gate * (1.0 - sigmoid_gate))
    ).astype(jnp.bfloat16)
    back_up = (back_hidden * activated).astype(jnp.bfloat16)
    step_gate = jnp.einsum("thd,hte->hde", key_split, back_gate, preferred_element_type=jnp.float32)
    step_up = jnp.einsum("thd,hte->hde", key_split, back_up, preferred_element_type=jnp.float32)
    step_down = jnp.einsum("hte,thf->hef", hidden, weighted, preferred_element_type=jnp.float32)
    return jnp.stack([step_gate, step_up, step_down])


def per_device(
    context_keys,
    context_values,
    context_queries,
    token_rates,
    w_gate,
    w_up,
    w_down,
    question_rows,
    question_count,
):
    head_count = w_gate.shape[0]
    head_size = w_gate.shape[1]
    matrix_count = 3 * head_count
    context_out = fast_apply(context_queries, w_gate, w_up, w_down)
    direction = directions(context_keys, context_values, token_rates, w_gate, w_up, w_down)
    flat_grads = direction.reshape(matrix_count, head_size * head_size)
    total = lax.psum(flat_grads, "ctx")
    norm_sizes = jnp.sqrt(jnp.sum(total * total, axis=1, keepdims=True))
    scaled = (total / (norm_sizes + 1e-06)).astype(jnp.bfloat16)
    iterate = scaled.reshape(matrix_count, head_size, head_size)
    for sweep_index in range(NS_STEPS):
        gram_matrix = jnp.einsum(
            "mij,mkj->mik", iterate, iterate, preferred_element_type=jnp.float32
        ).astype(jnp.bfloat16)
        gram_square = jnp.einsum(
            "mij,mjk->mik", gram_matrix, gram_matrix, preferred_element_type=jnp.float32
        )
        polynomial = (
            quintic_second * gram_matrix.astype(jnp.float32) + quintic_third * gram_square
        ).astype(jnp.bfloat16)
        product = jnp.einsum(
            "mij,mjk->mik", polynomial, iterate, preferred_element_type=jnp.float32
        )
        iterate = (quintic_first * iterate.astype(jnp.float32) + product).astype(jnp.bfloat16)
    previous = jnp.stack([w_gate, w_up, w_down]).astype(jnp.float32)
    moved = previous + iterate.reshape(3, head_count, head_size, head_size).astype(jnp.float32)
    col_norms = jnp.sqrt(jnp.sum(previous * previous, axis=2, keepdims=True))
    updated = (
        moved * col_norms / jnp.sqrt(jnp.sum(moved * moved, axis=2, keepdims=True) + 1e-06)
    ).astype(jnp.bfloat16)
    capacity = question_rows.shape[0]
    outputs = fast_apply(question_rows, updated[0], updated[1], updated[2])
    live_mask = jnp.arange(capacity, dtype=jnp.int32) < question_count[0]
    answers = jnp.where(live_mask[:, None], outputs, jnp.zeros_like(outputs))
    return (context_out, answers)


MESH = pl.DeviceIdType.MESH
PIECES = 2
ROWS = 2


def dot(a, b, contract=((1,), (0,))):
    return lax.dot_general(a, b, (contract, ((), ())), preferred_element_type=jnp.float32)


def read_memory(rows, gate, up, down):
    pre_gate = dot(rows, gate)
    pre_up = dot(rows, up)
    hidden = (pre_gate * jax.nn.sigmoid(pre_gate) * pre_up).astype(jnp.bfloat16)
    return dot(hidden, down).astype(jnp.bfloat16)


def memory_kernel(
    lines,
    keys_hbm, values_hbm, queries_hbm, rates_hbm, gate_hbm, up_hbm, down_hbm, questions_hbm,
    context_ref, answers_ref,
    key_in, weighted_in, weighted_out, values, rates_in, queries, gate, up, down, questions, acc, other_acc, twin_acc, twin_other, twin_sum, far, gathered,
    local_sem, key_send, key_recv, val_send, val_recv, sum_send, sum_recv,
    up_send, down_send, cross_send, pair_send, line_recv, pair_recv,
):
    heads, size, _ = gate.shape
    me = lax.axis_index("ctx")
    core, chip = me % ROWS, me // ROWS
    y, z = chip % ROWS, chip // ROWS
    half = 3 * size // ROWS
    near_lines = lines // 2
    first_line = z // near_lines * near_lines

    def opposite(line):
        return (line + near_lines) % lines

    def near(n):
        return first_line + (z + n) % near_lines

    twin = opposite(z) * ROWS + y
    piece = half // PIECES

    def device(a_chip, a_core):
        return {"ctx": a_chip * ROWS + a_core}

    def place(j):
        return (z // 2 + j // 2) % (lines // 2) * 2 + (z + j) % 2

    def columns(head):
        return pl.ds(pl.multiple_of(head * size, size), size)

    barrier = pltpu.get_barrier_semaphore()
    for j in range(lines):
        for dy in range(ROWS):
            if j or dy:
                peer = place(j) * ROWS + (y + dy) % ROWS
                pl.semaphore_signal(barrier, inc=1, device_id=device(peer, core), device_id_type=MESH)
    pl.semaphore_signal(barrier, inc=1, device_id=device(chip, 1 - core), device_id_type=MESH)

    loads = [
        pltpu.make_async_copy(src, dst, local_sem.at[i])
        for i, (src, dst) in enumerate([
            (rates_hbm, rates_in), (values_hbm, values),
            (keys_hbm.at[:, columns(chip)], key_in.at[chip]),
            (keys_hbm.at[:, columns(twin)], key_in.at[twin]),
            (queries_hbm, queries), (gate_hbm, gate), (up_hbm, up), (down_hbm, down),
            (questions_hbm, questions),
        ])
    ]
    for load in loads:
        load.start()

    loads[0].wait()
    loads[1].wait()
    rates = rates_in[...].T
    for head in range(heads):
        cols = slice(head * size, (head + 1) * size)
        weighted_out[head] = (
            rates[:, head:head + 1] * values[:, cols].astype(jnp.float32)
        ).astype(jnp.bfloat16)
    own_weighted = [
        pltpu.make_async_copy(weighted_out.at[head], weighted_in.at[head], local_sem.at[9 + i])
        for i, head in enumerate((chip, twin))
    ]

    pl.semaphore_wait(barrier, lines * ROWS)
    for load in own_weighted:
        load.start()

    def key_copy(head, to, slot):
        return pltpu.make_async_remote_copy(
            src_ref=keys_hbm.at[:, columns(head)], dst_ref=key_in.at[slot],
            send_sem=key_send.at[head], recv_sem=key_recv.at[slot],
            device_id=device(to, core), device_id_type=MESH)

    def val_copy(head, to, slot):
        return pltpu.make_async_remote_copy(
            src_ref=weighted_out.at[head], dst_ref=weighted_in.at[slot],
            send_sem=val_send.at[head], recv_sem=val_recv.at[slot],
            device_id=device(to, core), device_id_type=MESH)

    for side in (opposite, lambda line: line):
        for n in reversed(range(near_lines)):
            for dy in range(ROWS):
                if n or dy:
                    row = (y + dy) % ROWS
                    head = side(near(n)) * ROWS + row
                    slot = side(z) * ROWS + y
                    key_copy(head, near(n) * ROWS + row, slot).start()
                    val_copy(head, near(n) * ROWS + row, slot).start()

    for load in loads[2:8]:
        load.wait()

    @pl.loop(0, heads)
    def _(head):
        context_ref[:, columns(head)] = read_memory(
            queries[:, columns(head)], gate[head], up[head], down[head])

    for load in own_weighted:
        load.wait()

    def gradients(head, side, sums):
        sums[...] = jnp.zeros_like(sums)

        @pl.loop(0, near_lines)
        def _(n):
            accumulate(near(n), head, side(near(n)), sums)

    def accumulate(line, head, slots, sums):
        for row in range(ROWS):
            slot = slots * ROWS + row

            @pl.when(line * ROWS + row != chip)
            def _():
                key_copy(slot, chip, slot).wait_recv()
                val_copy(slot, chip, slot).wait_recv()

        pair = pl.ds(slots * ROWS, ROWS)
        key = key_in[pair].reshape(-1, size)
        weighted = weighted_in[pair].reshape(-1, size)
        pre_gate = dot(key, gate[head])
        pre_up = dot(key, up[head])
        back_hidden = dot(weighted, down[head], ((1,), (1,)))
        sigmoid = jax.nn.sigmoid(pre_gate)
        active = pre_gate * sigmoid
        hidden = (active * pre_up).astype(jnp.bfloat16)
        back_gate = (
            back_hidden * pre_up * sigmoid * (1.0 + pre_gate * (1.0 - sigmoid))
        ).astype(jnp.bfloat16)
        back_up = (back_hidden * active).astype(jnp.bfloat16)
        sums[0:size, :] += dot(key, back_gate, ((0,), (0,)))
        sums[size:2 * size, :] += dot(key, back_up, ((0,), (0,)))
        sums[2 * size:3 * size, :] += dot(hidden, weighted, ((0,), (0,)))

    def send(i, src, dst, to_chip, to_core):
        return pltpu.make_async_remote_copy(
            src_ref=src, dst_ref=dst, send_sem=sum_send.at[i], recv_sem=sum_recv.at[i],
            device_id=device(to_chip, to_core), device_id_type=MESH)

    def part_of(a_core):
        return pl.ds(pl.multiple_of(a_core * half, half), half)

    gradients(twin, opposite, twin_acc)
    fold = send(0, twin_acc.at[part_of(1 - core)], twin_other, chip, 1 - core)
    fold.start()
    fold.wait()
    twin_sum[...] = (twin_acc[part_of(core), :] + twin_other[...]).astype(jnp.bfloat16)
    across_half = send(1, twin_sum, far.at[part_of(core)], twin, core)
    across_half.start()

    gradients(chip, lambda line: line, acc)
    exchange = send(2, acc, other_acc, chip, 1 - core)
    exchange.start()
    exchange.wait()
    across_half.wait()
    share = send(3, far.at[part_of(core)], far.at[part_of(core)], chip, 1 - core)
    share.start()
    share.wait_send()
    send(3, far.at[part_of(1 - core)], far.at[part_of(1 - core)], chip, 1 - core).wait_recv()

    matrices = []
    for m in range(3):
        rows = slice(m * size, (m + 1) * size)
        total = (acc[rows, :] + other_acc[rows, :]) + far[rows, :].astype(jnp.float32)
        norm = jnp.sqrt(jnp.sum(total * total, keepdims=True))
        matrices.append((total / (norm + 1e-06)).astype(jnp.bfloat16))
    for _ in range(NS_STEPS):
        grams = [dot(x, x, ((1,), (1,))).astype(jnp.bfloat16) for x in matrices]
        polys = [
            (quintic_second * g.astype(jnp.float32) + quintic_third * dot(g, g)).astype(jnp.bfloat16)
            for g in grams
        ]
        matrices = [
            (quintic_first * x.astype(jnp.float32) + dot(p, x)).astype(jnp.bfloat16)
            for p, x in zip(polys, matrices)
        ]
    for m, (initial, x) in enumerate(zip((gate, up, down), matrices)):
        previous = initial[chip].astype(jnp.float32)
        moved = previous + x.astype(jnp.float32)
        norms = jnp.sqrt(jnp.sum(previous * previous, axis=0, keepdims=True))
        gathered[chip, m * size:(m + 1) * size, :] = (
            moved * norms / jnp.sqrt(jnp.sum(moved * moved, axis=0, keepdims=True) + 1e-06)
        ).astype(jnp.bfloat16)

    def hop(origin, p, part, send, recv, to_chip, to_core):
        rows = pl.ds(pl.multiple_of(part * half + p * piece, piece), piece)
        block = gathered.at[origin, rows]
        slot = origin * PIECES + p
        return pltpu.make_async_remote_copy(
            src_ref=block, dst_ref=block, send_sem=send.at[slot], recv_sem=recv.at[slot],
            device_id=device(to_chip, to_core), device_id_type=MESH)

    def hop_up(origin, p):
        return hop(origin, p, core, up_send, line_recv, chip + ROWS, core)

    def hop_down(origin, p):
        return hop(origin, p, core, down_send, line_recv, chip - ROWS, core)

    def hop_cross(origin, p):
        return hop(origin, p, core, cross_send, line_recv, z * ROWS + 1 - y, core)

    def hop_pair(origin, p):
        return hop(origin, p, core, pair_send, pair_recv, chip, 1 - core)

    def from_pair(origin, p):
        return hop(origin, p, 1 - core, pair_send, pair_recv, chip, 1 - core)

    def answer(origin):
        answers_ref[:, columns(origin)] = read_memory(
            questions[:, columns(origin)],
            gathered[origin, 0:size, :],
            gathered[origin, size:2 * size, :],
            gathered[origin, 2 * size:3 * size, :])

    def early(line):
        return (core == 0) & ((line == 0) | (line == lines - 1))

    def late(line):
        return jnp.logical_not(early(line))

    has_up, has_down = z + 1 < lines, z > 0

    def mine(line):
        return line * ROWS + y

    def across(line):
        return line * ROWS + 1 - y

    for p in range(PIECES):
        hop_cross(chip, p).start()
        pl.when(has_up)(lambda: hop_up(chip, p).start())
        pl.when(has_down)(lambda: hop_down(chip, p).start())

    @pl.when(early(z))
    def _():
        for p in range(PIECES):
            hop_cross(across(z), p).wait_recv()
            pl.when(has_up)(lambda: hop_up(across(z), p).start())
            pl.when(has_down)(lambda: hop_down(across(z), p).start())
            hop_pair(across(z), p).start()

    loads[8].wait()
    answer(chip)

    def along(line, has_next, next_hop):
        for p in range(PIECES):
            origin = mine(line)
            hop_cross(origin, p).wait_recv()
            pl.when(has_next)(lambda: next_hop(origin, p).start())
            pl.when(late(line))(lambda: hop_cross(origin, p).start())
            hop_pair(origin, p).start()

        @pl.when(early(line))
        def _():
            for p in range(PIECES):
                hop_cross(across(line), p).wait_recv()
                pl.when(has_next)(lambda: next_hop(across(line), p).start())
                hop_pair(across(line), p).start()

    def crossed(line):
        @pl.when(late(line))
        def _():
            for p in range(PIECES):
                hop_cross(across(line), p).wait_recv()
                hop_pair(across(line), p).start()

    def finish(origin):
        for p in range(PIECES):
            from_pair(origin, p).wait_recv()
        answer(origin)

    @pl.loop(1, lines + 2)
    def _(k):
        pl.when(z - k >= 0)(lambda: along(z - k, has_up, hop_up))
        pl.when(z + k < lines)(lambda: along(z + k, has_down, hop_down))
        step = k - 1
        last = k - 2
        pl.when(z - step >= 0)(lambda: crossed(z - step))
        pl.when((step > 0) & (z + step < lines))(lambda: crossed(z + step))
        pl.when((step > 0) & (z - step >= 0))(lambda: finish(mine(z - step)))
        pl.when((step > 0) & (z + step < lines))(lambda: finish(mine(z + step)))
        pl.when((last >= 0) & (z - last >= 0))(lambda: finish(across(z - last)))
        pl.when((last > 0) & (z + last < lines))(lambda: finish(across(z + last)))

    @pl.loop(0, lines)
    def _(line):
        goes_up = (line <= z) & has_up
        goes_down = (line >= z) & has_down
        for row in range(ROWS):
            head = line * ROWS + row

            @pl.when((head != chip) & (head != twin))
            def _():
                key_copy(head, chip, head).wait_send()
                val_copy(head, chip, head).wait_send()

        for p in range(PIECES):
            pl.when(goes_up & early(line))(lambda: hop_up(across(line), p).wait_send())
            pl.when(goes_down & early(line))(lambda: hop_down(across(line), p).wait_send())
            pl.when(goes_up)(lambda: hop_up(mine(line), p).wait_send())
            pl.when(goes_down)(lambda: hop_down(mine(line), p).wait_send())
            pl.when(late(line) | (line == z))(lambda: hop_cross(mine(line), p).wait_send())
            hop_pair(across(line), p).wait_send()
            pl.when(line != z)(lambda: hop_pair(mine(line), p).wait_send())


def head_per_chip(
    lines,
    context_keys,
    context_values,
    context_queries,
    token_rates,
    w_gate,
    w_up,
    w_down,
    question_rows,
    question_count,
):
    heads, size, _ = w_gate.shape
    tokens, width = context_keys.shape
    capacity = question_rows.shape[0]
    vmem = pl.BlockSpec(memory_space=pltpu.VMEM)
    sem = pltpu.SemaphoreType.DMA
    half_type = jnp.bfloat16
    context_out, outputs = pl.pallas_call(
        functools.partial(memory_kernel, lines),
        out_shape=(
            jax.ShapeDtypeStruct((tokens, width), half_type),
            jax.ShapeDtypeStruct((capacity, width), half_type),
        ),
        in_specs=[pl.BlockSpec(memory_space=pltpu.HBM)] * 8,
        out_specs=(vmem, vmem),
        scratch_shapes=[
            pltpu.VMEM((heads, tokens, size), half_type),
            pltpu.VMEM((heads, tokens, size), half_type),
            pltpu.VMEM((heads, tokens, size), half_type),
            pltpu.VMEM((tokens, width), half_type),
            pltpu.VMEM((heads, tokens), jnp.float32),
            pltpu.VMEM((tokens, width), half_type),
            pltpu.VMEM((heads, size, size), half_type),
            pltpu.VMEM((heads, size, size), half_type),
            pltpu.VMEM((heads, size, size), half_type),
            pltpu.VMEM((capacity, width), half_type),
            *[pltpu.VMEM((3 * size, size), jnp.float32)] * 3,
            pltpu.VMEM((3 * size // ROWS, size), jnp.float32),
            pltpu.VMEM((3 * size // ROWS, size), half_type),
            pltpu.VMEM((3 * size, size), half_type),
            pltpu.VMEM((heads, 3 * size, size), half_type),
            sem((11,)),
            sem((heads,)), sem((heads,)), sem((heads,)), sem((heads,)),
            sem((4,)), sem((4,)),
            *[sem((heads * PIECES,))] * 6,
        ],
        compiler_params=pltpu.CompilerParams(
            collective_id=0, has_side_effects=True, vmem_limit_bytes=48 * 1024 * 1024
        ),
    )(*(
        pltpu.with_memory_space_constraint(array, pltpu.HBM)
        for array in (
            context_keys, context_values, context_queries, token_rates,
            w_gate, w_up, w_down, question_rows,
        )
    ))
    live_mask = jnp.arange(capacity, dtype=jnp.int32) < question_count[0]
    return context_out, jnp.where(live_mask[:, None], outputs, jnp.zeros_like(outputs))


def solution(mesh):
    members = mesh.shape["ctx"]
    lines = members // (ROWS * ROWS)

    def body(*arrays):
        heads = arrays[4].shape[0]
        if members == ROWS * heads and lines % 2 == 0:
            return head_per_chip(lines, *arrays)
        return per_device(*arrays)

    return jax.shard_map(
        body,
        mesh=mesh,
        in_specs=(
            P(("groups", "ctx"), None),
            P(("groups", "ctx"), None),
            P(("groups", "ctx"), None),
            P(None, ("groups", "ctx")),
            P(),
            P(),
            P(),
            P(("groups", "ctx"), None),
            P(("groups", "ctx")),
        ),
        out_specs=(P(("groups", "ctx"), None), P(("groups", "ctx"), None)),
        check_vma=False,
    )
```

```python
import functools

import jax
import jax.numpy as jnp
from jax import lax
from jax.experimental import pallas as pl
from jax.experimental.pallas import tpu as pltpu
from jax.sharding import PartitionSpec as P

NS_STEPS = 3


quintic_first = 3.4445
quintic_second = -4.775
quintic_third = 2.0315


def fast_apply(in_rows, w_gate, w_up, w_down):
    head_count = w_gate.shape[0]
    head_size = w_gate.shape[1]
    row_split = in_rows.reshape(in_rows.shape[0], head_count, head_size)
    pre_gate = jnp.einsum("thd,hde->hte", row_split, w_gate, preferred_element_type=jnp.float32)
    pre_up = jnp.einsum("thd,hde->hte", row_split, w_up, preferred_element_type=jnp.float32)
    hidden = (jax.nn.silu(pre_gate) * pre_up).astype(jnp.bfloat16)
    outputs = jnp.einsum("hte,hef->thf", hidden, w_down, preferred_element_type=jnp.float32)
    return outputs.reshape(in_rows.shape[0], head_count * head_size).astype(jnp.bfloat16)


def directions(context_keys, context_values, token_rates, w_gate, w_up, w_down):
    tok_rows = context_keys.shape[0]
    head_count = w_gate.shape[0]
    head_size = w_gate.shape[1]
    key_split = context_keys.reshape(tok_rows, head_count, head_size)
    value_split = context_values.reshape(tok_rows, head_count, head_size)
    pre_gate = jnp.einsum("thd,hde->hte", key_split, w_gate, preferred_element_type=jnp.float32)
    pre_up = jnp.einsum("thd,hde->hte", key_split, w_up, preferred_element_type=jnp.float32)
    sigmoid_gate = jax.nn.sigmoid(pre_gate)
    activated = pre_gate * sigmoid_gate
    hidden = (activated * pre_up).astype(jnp.bfloat16)
    weighted = (token_rates.T[:, :, None] * value_split).astype(jnp.bfloat16)
    back_hidden = jnp.einsum("thf,hef->hte", weighted, w_down, preferred_element_type=jnp.float32)
    back_gate = (
        back_hidden * pre_up * sigmoid_gate * (1.0 + pre_gate * (1.0 - sigmoid_gate))
    ).astype(jnp.bfloat16)
    back_up = (back_hidden * activated).astype(jnp.bfloat16)
    step_gate = jnp.einsum("thd,hte->hde", key_split, back_gate, preferred_element_type=jnp.float32)
    step_up = jnp.einsum("thd,hte->hde", key_split, back_up, preferred_element_type=jnp.float32)
    step_down = jnp.einsum("hte,thf->hef", hidden, weighted, preferred_element_type=jnp.float32)
    return jnp.stack([step_gate, step_up, step_down])


def per_device(
    context_keys,
    context_values,
    context_queries,
    token_rates,
    w_gate,
    w_up,
    w_down,
    question_rows,
    question_count,
):
    head_count = w_gate.shape[0]
    head_size = w_gate.shape[1]
    matrix_count = 3 * head_count
    context_out = fast_apply(context_queries, w_gate, w_up, w_down)
    direction = directions(context_keys, context_values, token_rates, w_gate, w_up, w_down)
    flat_grads = direction.reshape(matrix_count, head_size * head_size)
    total = lax.psum(flat_grads, "ctx")
    norm_sizes = jnp.sqrt(jnp.sum(total * total, axis=1, keepdims=True))
    scaled = (total / (norm_sizes + 1e-06)).astype(jnp.bfloat16)
    iterate = scaled.reshape(matrix_count, head_size, head_size)
    for sweep_index in range(NS_STEPS):
        gram_matrix = jnp.einsum(
            "mij,mkj->mik", iterate, iterate, preferred_element_type=jnp.float32
        ).astype(jnp.bfloat16)
        gram_square = jnp.einsum(
            "mij,mjk->mik", gram_matrix, gram_matrix, preferred_element_type=jnp.float32
        )
        polynomial = (
            quintic_second * gram_matrix.astype(jnp.float32) + quintic_third * gram_square
        ).astype(jnp.bfloat16)
        product = jnp.einsum(
            "mij,mjk->mik", polynomial, iterate, preferred_element_type=jnp.float32
        )
        iterate = (quintic_first * iterate.astype(jnp.float32) + product).astype(jnp.bfloat16)
    previous = jnp.stack([w_gate, w_up, w_down]).astype(jnp.float32)
    moved = previous + iterate.reshape(3, head_count, head_size, head_size).astype(jnp.float32)
    col_norms = jnp.sqrt(jnp.sum(previous * previous, axis=2, keepdims=True))
    updated = (
        moved * col_norms / jnp.sqrt(jnp.sum(moved * moved, axis=2, keepdims=True) + 1e-06)
    ).astype(jnp.bfloat16)
    capacity = question_rows.shape[0]
    outputs = fast_apply(question_rows, updated[0], updated[1], updated[2])
    live_mask = jnp.arange(capacity, dtype=jnp.int32) < question_count[0]
    answers = jnp.where(live_mask[:, None], outputs, jnp.zeros_like(outputs))
    return (context_out, answers)


MESH = pl.DeviceIdType.MESH
PIECES = 2
ROWS = 2


def dot(a, b, contract=((1,), (0,))):
    return lax.dot_general(a, b, (contract, ((), ())), preferred_element_type=jnp.float32)


def read_memory(rows, gate, up, down):
    pre_gate = dot(rows, gate)
    pre_up = dot(rows, up)
    hidden = (pre_gate * jax.nn.sigmoid(pre_gate) * pre_up).astype(jnp.bfloat16)
    return dot(hidden, down).astype(jnp.bfloat16)


def memory_kernel(
    lines,
    keys_hbm, values_hbm, queries_hbm, rates_hbm, gate_hbm, up_hbm, down_hbm, questions_hbm,
    context_ref, answers_ref,
    key_in, weighted_in, weighted_out, values, rates_in, queries, gate, up, down, questions, acc, other_acc, twin_acc, twin_other, twin_sum, far, gathered,
    local_sem, key_send, key_recv, val_send, val_recv, sum_send, sum_recv,
    up_send, down_send, cross_send, pair_send, line_recv, pair_recv,
):
    heads, size, _ = gate.shape
    me = lax.axis_index("ctx")
    core, chip = me % ROWS, me // ROWS
    y, z = chip % ROWS, chip // ROWS
    half = 3 * size // ROWS
    near_lines = lines // 2
    first_line = z // near_lines * near_lines

    def opposite(line):
        return (line + near_lines) % lines

    def near(n):
        return first_line + (z + n) % near_lines

    twin = opposite(z) * ROWS + y
    piece = half // PIECES

    def device(a_chip, a_core):
        return {"ctx": a_chip * ROWS + a_core}

    def place(j):
        return (z // 2 + j // 2) % (lines // 2) * 2 + (z + j) % 2

    def columns(head):
        return pl.ds(pl.multiple_of(head * size, size), size)

    barrier = pltpu.get_barrier_semaphore()
    for j in range(lines):
        for dy in range(ROWS):
            if j or dy:
                peer = place(j) * ROWS + (y + dy) % ROWS
                pl.semaphore_signal(barrier, inc=1, device_id=device(peer, core), device_id_type=MESH)
    pl.semaphore_signal(barrier, inc=1, device_id=device(chip, 1 - core), device_id_type=MESH)

    loads = [
        pltpu.make_async_copy(src, dst, local_sem.at[i])
        for i, (src, dst) in enumerate([
            (rates_hbm, rates_in), (values_hbm, values),
            (keys_hbm.at[:, columns(chip)], key_in.at[chip]),
            (keys_hbm.at[:, columns(twin)], key_in.at[twin]),
            (queries_hbm, queries), (gate_hbm, gate), (up_hbm, up), (down_hbm, down),
            (questions_hbm, questions),
        ])
    ]
    for load in loads:
        load.start()

    loads[0].wait()
    loads[1].wait()
    rates = rates_in[...].T
    for head in range(heads):
        cols = slice(head * size, (head + 1) * size)
        weighted_out[head] = (
            rates[:, head:head + 1] * values[:, cols].astype(jnp.float32)
        ).astype(jnp.bfloat16)
    own_weighted = [
        pltpu.make_async_copy(weighted_out.at[head], weighted_in.at[head], local_sem.at[9 + i])
        for i, head in enumerate((chip, twin))
    ]

    pl.semaphore_wait(barrier, lines * ROWS)
    for load in own_weighted:
        load.start()

    def key_copy(head, to, slot):
        return pltpu.make_async_remote_copy(
            src_ref=keys_hbm.at[:, columns(head)], dst_ref=key_in.at[slot],
            send_sem=key_send.at[head], recv_sem=key_recv.at[slot],
            device_id=device(to, core), device_id_type=MESH)

    def val_copy(head, to, slot):
        return pltpu.make_async_remote_copy(
            src_ref=weighted_out.at[head], dst_ref=weighted_in.at[slot],
            send_sem=val_send.at[head], recv_sem=val_recv.at[slot],
            device_id=device(to, core), device_id_type=MESH)

    for side in (opposite, lambda line: line):
        for n in reversed(range(near_lines)):
            for dy in range(ROWS):
                if n or dy:
                    row = (y + dy) % ROWS
                    head = side(near(n)) * ROWS + row
                    slot = side(z) * ROWS + y
                    key_copy(head, near(n) * ROWS + row, slot).start()
                    val_copy(head, near(n) * ROWS + row, slot).start()

    for load in loads[2:8]:
        load.wait()

    @pl.loop(0, heads)
    def _(head):
        context_ref[:, columns(head)] = read_memory(
            queries[:, columns(head)], gate[head], up[head], down[head])

    for load in own_weighted:
        load.wait()

    def gradients(head, side, sums):
        sums[...] = jnp.zeros_like(sums)

        @pl.loop(0, near_lines)
        def _(n):
            accumulate(near(n), head, side(near(n)), sums)

    def accumulate(line, head, slots, sums):
        for row in range(ROWS):
            slot = slots * ROWS + row

            @pl.when(line * ROWS + row != chip)
            def _():
                key_copy(slot, chip, slot).wait_recv()
                val_copy(slot, chip, slot).wait_recv()

        pair = pl.ds(slots * ROWS, ROWS)
        key = key_in[pair].reshape(-1, size)
        weighted = weighted_in[pair].reshape(-1, size)
        pre_gate = dot(key, gate[head])
        pre_up = dot(key, up[head])
        back_hidden = dot(weighted, down[head], ((1,), (1,)))
        sigmoid = jax.nn.sigmoid(pre_gate)
        active = pre_gate * sigmoid
        hidden = (active * pre_up).astype(jnp.bfloat16)
        back_gate = (
            back_hidden * pre_up * sigmoid * (1.0 + pre_gate * (1.0 - sigmoid))
        ).astype(jnp.bfloat16)
        back_up = (back_hidden * active).astype(jnp.bfloat16)
        sums[0:size, :] += dot(key, back_gate, ((0,), (0,)))
        sums[size:2 * size, :] += dot(key, back_up, ((0,), (0,)))
        sums[2 * size:3 * size, :] += dot(hidden, weighted, ((0,), (0,)))

    def send(i, src, dst, to_chip, to_core):
        return pltpu.make_async_remote_copy(
            src_ref=src, dst_ref=dst, send_sem=sum_send.at[i], recv_sem=sum_recv.at[i],
            device_id=device(to_chip, to_core), device_id_type=MESH)

    third = half // 3

    def part_of(a_core, p):
        return pl.ds(pl.multiple_of(a_core * half + p * third, third), third)

    gradients(twin, opposite, twin_acc)
    folds = [
        send(p, twin_acc.at[part_of(1 - core, p)], twin_other.at[part_of(0, p)], chip, 1 - core)
        for p in range(3)
    ]
    for fold in folds:
        fold.start()
    crossings = []
    for p in range(3):
        folds[p].wait_recv()
        twin_sum[part_of(0, p), :] = (
            twin_acc[part_of(core, p), :] + twin_other[part_of(0, p), :]
        ).astype(jnp.bfloat16)
        crossings.append(send(3 + p, twin_sum.at[part_of(0, p)], far.at[part_of(core, p)], twin, core))
        crossings[p].start()

    gradients(chip, lambda line: line, acc)
    exchange = send(9, acc, other_acc, chip, 1 - core)
    exchange.start()
    exchange.wait()
    shares = []
    for p in range(3):
        crossings[p].wait_recv()
        shares.append(
            send(6 + p, far.at[part_of(core, p)], far.at[part_of(core, p)], chip, 1 - core))
        shares[p].start()
    for p in range(3):
        send(6 + p, far.at[part_of(1 - core, p)], far.at[part_of(1 - core, p)], chip, 1 - core).wait_recv()
        for copy in (folds[p], crossings[p], shares[p]):
            copy.wait_send()

    matrices = []
    for m in range(3):
        rows = slice(m * size, (m + 1) * size)
        total = (acc[rows, :] + other_acc[rows, :]) + far[rows, :].astype(jnp.float32)
        norm = jnp.sqrt(jnp.sum(total * total, keepdims=True))
        matrices.append((total / (norm + 1e-06)).astype(jnp.bfloat16))
    for _ in range(NS_STEPS):
        grams = [dot(x, x, ((1,), (1,))).astype(jnp.bfloat16) for x in matrices]
        polys = [
            (quintic_second * g.astype(jnp.float32) + quintic_third * dot(g, g)).astype(jnp.bfloat16)
            for g in grams
        ]
        matrices = [
            (quintic_first * x.astype(jnp.float32) + dot(p, x)).astype(jnp.bfloat16)
            for p, x in zip(polys, matrices)
        ]
    for m, (initial, x) in enumerate(zip((gate, up, down), matrices)):
        previous = initial[chip].astype(jnp.float32)
        moved = previous + x.astype(jnp.float32)
        norms = jnp.sqrt(jnp.sum(previous * previous, axis=0, keepdims=True))
        gathered[chip, m * size:(m + 1) * size, :] = (
            moved * norms / jnp.sqrt(jnp.sum(moved * moved, axis=0, keepdims=True) + 1e-06)
        ).astype(jnp.bfloat16)

    def hop(origin, p, part, send, recv, to_chip, to_core):
        rows = pl.ds(pl.multiple_of(part * half + p * piece, piece), piece)
        block = gathered.at[origin, rows]
        slot = origin * PIECES + p
        return pltpu.make_async_remote_copy(
            src_ref=block, dst_ref=block, send_sem=send.at[slot], recv_sem=recv.at[slot],
            device_id=device(to_chip, to_core), device_id_type=MESH)

    def hop_up(origin, p):
        return hop(origin, p, core, up_send, line_recv, chip + ROWS, core)

    def hop_down(origin, p):
        return hop(origin, p, core, down_send, line_recv, chip - ROWS, core)

    def hop_cross(origin, p):
        return hop(origin, p, core, cross_send, line_recv, z * ROWS + 1 - y, core)

    def hop_pair(origin, p):
        return hop(origin, p, core, pair_send, pair_recv, chip, 1 - core)

    def from_pair(origin, p):
        return hop(origin, p, 1 - core, pair_send, pair_recv, chip, 1 - core)

    def answer(origin):
        answers_ref[:, columns(origin)] = read_memory(
            questions[:, columns(origin)],
            gathered[origin, 0:size, :],
            gathered[origin, size:2 * size, :],
            gathered[origin, 2 * size:3 * size, :])

    def early(line):
        return (core == 0) & ((line == 0) | (line == lines - 1))

    def late(line):
        return jnp.logical_not(early(line))

    has_up, has_down = z + 1 < lines, z > 0

    def mine(line):
        return line * ROWS + y

    def across(line):
        return line * ROWS + 1 - y

    for p in range(PIECES):
        hop_cross(chip, p).start()
        pl.when(has_up)(lambda: hop_up(chip, p).start())
        pl.when(has_down)(lambda: hop_down(chip, p).start())

    @pl.when(early(z))
    def _():
        for p in range(PIECES):
            hop_cross(across(z), p).wait_recv()
            pl.when(has_up)(lambda: hop_up(across(z), p).start())
            pl.when(has_down)(lambda: hop_down(across(z), p).start())
            hop_pair(across(z), p).start()

    loads[8].wait()
    answer(chip)

    def along(line, has_next, next_hop):
        for p in range(PIECES):
            origin = mine(line)
            hop_cross(origin, p).wait_recv()
            pl.when(has_next)(lambda: next_hop(origin, p).start())
            pl.when(late(line))(lambda: hop_cross(origin, p).start())
            hop_pair(origin, p).start()

        @pl.when(early(line))
        def _():
            for p in range(PIECES):
                hop_cross(across(line), p).wait_recv()
                pl.when(has_next)(lambda: next_hop(across(line), p).start())
                hop_pair(across(line), p).start()

    def crossed(line):
        @pl.when(late(line))
        def _():
            for p in range(PIECES):
                hop_cross(across(line), p).wait_recv()
                hop_pair(across(line), p).start()

    def finish(origin):
        for p in range(PIECES):
            from_pair(origin, p).wait_recv()
        answer(origin)

    @pl.loop(1, lines + 2)
    def _(k):
        pl.when(z - k >= 0)(lambda: along(z - k, has_up, hop_up))
        pl.when(z + k < lines)(lambda: along(z + k, has_down, hop_down))
        step = k - 1
        last = k - 2
        pl.when(z - step >= 0)(lambda: crossed(z - step))
        pl.when((step > 0) & (z + step < lines))(lambda: crossed(z + step))
        pl.when((step > 0) & (z - step >= 0))(lambda: finish(mine(z - step)))
        pl.when((step > 0) & (z + step < lines))(lambda: finish(mine(z + step)))
        pl.when((last >= 0) & (z - last >= 0))(lambda: finish(across(z - last)))
        pl.when((last > 0) & (z + last < lines))(lambda: finish(across(z + last)))

    @pl.loop(0, lines)
    def _(line):
        goes_up = (line <= z) & has_up
        goes_down = (line >= z) & has_down
        for row in range(ROWS):
            head = line * ROWS + row

            @pl.when((head != chip) & (head != twin))
            def _():
                key_copy(head, chip, head).wait_send()
                val_copy(head, chip, head).wait_send()

        for p in range(PIECES):
            pl.when(goes_up & early(line))(lambda: hop_up(across(line), p).wait_send())
            pl.when(goes_down & early(line))(lambda: hop_down(across(line), p).wait_send())
            pl.when(goes_up)(lambda: hop_up(mine(line), p).wait_send())
            pl.when(goes_down)(lambda: hop_down(mine(line), p).wait_send())
            pl.when(late(line) | (line == z))(lambda: hop_cross(mine(line), p).wait_send())
            hop_pair(across(line), p).wait_send()
            pl.when(line != z)(lambda: hop_pair(mine(line), p).wait_send())


def head_per_chip(
    lines,
    context_keys,
    context_values,
    context_queries,
    token_rates,
    w_gate,
    w_up,
    w_down,
    question_rows,
    question_count,
):
    heads, size, _ = w_gate.shape
    tokens, width = context_keys.shape
    capacity = question_rows.shape[0]
    vmem = pl.BlockSpec(memory_space=pltpu.VMEM)
    sem = pltpu.SemaphoreType.DMA
    half_type = jnp.bfloat16
    context_out, outputs = pl.pallas_call(
        functools.partial(memory_kernel, lines),
        out_shape=(
            jax.ShapeDtypeStruct((tokens, width), half_type),
            jax.ShapeDtypeStruct((capacity, width), half_type),
        ),
        in_specs=[pl.BlockSpec(memory_space=pltpu.HBM)] * 8,
        out_specs=(vmem, vmem),
        scratch_shapes=[
            pltpu.VMEM((heads, tokens, size), half_type),
            pltpu.VMEM((heads, tokens, size), half_type),
            pltpu.VMEM((heads, tokens, size), half_type),
            pltpu.VMEM((tokens, width), half_type),
            pltpu.VMEM((heads, tokens), jnp.float32),
            pltpu.VMEM((tokens, width), half_type),
            pltpu.VMEM((heads, size, size), half_type),
            pltpu.VMEM((heads, size, size), half_type),
            pltpu.VMEM((heads, size, size), half_type),
            pltpu.VMEM((capacity, width), half_type),
            *[pltpu.VMEM((3 * size, size), jnp.float32)] * 3,
            pltpu.VMEM((3 * size // ROWS, size), jnp.float32),
            pltpu.VMEM((3 * size // ROWS, size), half_type),
            pltpu.VMEM((3 * size, size), half_type),
            pltpu.VMEM((heads, 3 * size, size), half_type),
            sem((11,)),
            sem((heads,)), sem((heads,)), sem((heads,)), sem((heads,)),
            sem((10,)), sem((10,)),
            *[sem((heads * PIECES,))] * 6,
        ],
        compiler_params=pltpu.CompilerParams(
            collective_id=0, has_side_effects=True, vmem_limit_bytes=48 * 1024 * 1024
        ),
    )(*(
        pltpu.with_memory_space_constraint(array, pltpu.HBM)
        for array in (
            context_keys, context_values, context_queries, token_rates,
            w_gate, w_up, w_down, question_rows,
        )
    ))
    live_mask = jnp.arange(capacity, dtype=jnp.int32) < question_count[0]
    return context_out, jnp.where(live_mask[:, None], outputs, jnp.zeros_like(outputs))


def solution(mesh):
    members = mesh.shape["ctx"]
    lines = members // (ROWS * ROWS)

    def body(*arrays):
        heads = arrays[4].shape[0]
        if members == ROWS * heads and lines % 2 == 0:
            return head_per_chip(lines, *arrays)
        return per_device(*arrays)

    return jax.shard_map(
        body,
        mesh=mesh,
        in_specs=(
            P(("groups", "ctx"), None),
            P(("groups", "ctx"), None),
            P(("groups", "ctx"), None),
            P(None, ("groups", "ctx")),
            P(),
            P(),
            P(),
            P(("groups", "ctx"), None),
            P(("groups", "ctx")),
        ),
        out_specs=(P(("groups", "ctx"), None), P(("groups", "ctx"), None)),
        check_vma=False,
    )
```
